32 devices in a mesh: dp: 8 (over y, x, core), space: 4 (over z).
Axes of the slice: x: 2, y: 2, z: 4, core: 2. Of those that a mesh axis runs over, the one named last changes fastest.
Arguments:
- features: bfloat16 [8, 32, 16, 512], P('dp', 'space'), may hold values from -48 to 48
- cotangent: bfloat16 [8, 32, 16, 512], P('dp', 'space'), may hold values from -6 to 6
- dw_kernel: float32 [7, 7, 512], replicated, may hold values from -0.875 to 0.875
- ln_gain: float32 [512], replicated, may hold values from 0.1 to 1.9
- ln_bias: float32 [512], replicated, may hold values from -3 to 3
- layer_scale: float32 [512], replicated, may hold values from 0.3 to 3
- w_up: bfloat16 [512, 2048], P('dp'), may hold values from -0.25 to 0.25
- w_down: bfloat16 [2048, 512], P('dp'), may hold values from -0.125 to 0.125
Outputs:
- result: bfloat16 [8, 32, 16, 512], P('dp', 'space')
- d_features: float32 [8, 32, 16, 512], P('dp', 'space')
- d_w_up: float32 [512, 2048], P('dp', 'space')
- d_w_down: float32 [2048, 512], P('space', 'dp')
- d_kernel: float32 [7, 7, 512], replicated
- d_gain: float32 [512], replicated
- d_bias: float32 [512], replicated
- d_scale: float32 [512], replicated
The draws below stay inside these ranges and needn't reach their ends.
All inputs are finite; a program needn't handle non-finite values.
Results may differ from the reference program's by a relative error of at most 0.0065.
Values may be sent and summed in bfloat16 or wider, within the bound.
A program may use at most 64 MiB of HBM per device.

```python
import math
import jax
import jax.numpy as jnp
from jax import lax

D = 512
FF = 2048
KW = 7
COLS = 16
REGIONS = 8
REGION_ROWS = 32
N_DP = 8


def draw_features(key, part):
    base_key, chan_key, pixel_key = jax.random.split(key, 3)
    shape = (REGIONS, REGION_ROWS, COLS, D)
    channel_scale = jnp.exp(jax.random.uniform(chan_key, (D,), jnp.float32, jnp.log(0.3), jnp.log(3.0)))
    pixel_scale = jnp.exp(jax.random.uniform(pixel_key, (REGIONS, REGION_ROWS, COLS, 1), jnp.float32, jnp.log(0.4), jnp.log(4.0)))
    base = jnp.clip(jax.random.normal(base_key, shape, jnp.float32), -4.0, 4.0)
    return (base * channel_scale * pixel_scale).astype(jnp.bfloat16)


def level_of(stream_key, extent, pieces, least, high):
    def one(axis_at, parts):
        steps = jax.random.uniform(jax.random.fold_in(jax.random.fold_in(stream_key, 6), axis_at), (parts,), jnp.float32, least / len(pieces), high / len(pieces))
        return jnp.repeat(jnp.exp(steps), extent[axis_at] // parts).reshape((-1,) + (1,) * (len(extent) - axis_at - 1))

    level = one(*pieces[0])
    for cut in pieces[1:]:
        level = level * one(*cut)
    return level


def noise(stream_key, shape, width, limit, cuts=(), held_as=jnp.bfloat16):
    drawn = width * jax.random.normal(stream_key, shape, jnp.float32)
    if cuts:
        drawn = drawn * level_of(stream_key, shape, cuts, -0.22, 0.18)
    return jnp.clip(drawn, -limit, limit).astype(held_as)


def setup_inputs(seed: int = 0) -> dict:
    key_list = jax.random.split(jax.random.key(seed), 9)
    return {
        "features": draw_features(jax.random.fold_in(key_list[8], 71), 0),
        "cotangent": noise(key_list[1], (REGIONS, REGION_ROWS, COLS, D), 1.0, 6.0, ((0, 8), (1, 4))),
        "dw_kernel": noise(key_list[2], (KW, KW, D), (KW * KW) ** -0.5, 0.875, (), jnp.float32),
        "ln_gain": jnp.clip(1.0 + 0.18 * jax.random.normal(key_list[3], (D,), jnp.float32), 0.1, 1.9),
        "ln_bias": noise(key_list[4], (D,), 0.5, 3.0, (), jnp.float32),
        "layer_scale": jnp.clip(jnp.exp(jax.random.uniform(key_list[5], (D,), jnp.float32, math.log(0.3), math.log(3.0))), 0.3, 3.0),
        "w_up": noise(key_list[6], (D, FF), D ** -0.5, 0.25, ((0, 8),)),
        "w_down": noise(key_list[7], (FF, D), FF ** -0.5, 0.125, ((0, 8),)),
    }


def gelu_pair(preact):
    cumulative = 0.5 * (1.0 + jax.scipy.special.erf(preact * (1.0 / math.sqrt(2.0))))
    density = jnp.exp(-0.5 * preact * preact) * (1.0 / math.sqrt(2.0 * math.pi))
    return (preact * cumulative, cumulative + preact * density)

def depthwise(padded, kernel, num_rows, num_cols):
    summed = jnp.zeros((num_rows, num_cols, padded.shape[-1]), jnp.float32)
    for row_off in range(kernel.shape[0]):
        for col_off in range(kernel.shape[1]):
            summed = summed + kernel[row_off, col_off] * padded[row_off:row_off + num_rows, col_off:col_off + num_cols]
    return summed

def kernel_grad(padded, upstream):
    num_rows, num_cols = (upstream.shape[0], upstream.shape[1])
    entries = []
    for row_off in range(KW):
        for col_off in range(KW):
            window = padded[row_off:row_off + num_rows, col_off:col_off + num_cols]
            entries.append(lax.optimization_barrier(jnp.sum(window * upstream, axis=(0, 1))))
    return jnp.stack(entries).reshape(KW, KW, upstream.shape[-1])

def normalize(conv_out, ln_gain, ln_bias):
    center = conv_out - lax.optimization_barrier(jnp.mean(conv_out, axis=-1, keepdims=True))
    inverse = lax.rsqrt(lax.optimization_barrier(jnp.mean(center * center, axis=-1, keepdims=True)) + 1e-06)
    scaled = center * inverse
    return (scaled, inverse, (scaled * ln_gain + ln_bias).astype(jnp.bfloat16))

def norm_back(d_norm, scaled, inverse, ln_gain):
    d_hat = d_norm * ln_gain
    first = lax.optimization_barrier(jnp.mean(d_hat, axis=-1, keepdims=True))
    second = lax.optimization_barrier(jnp.mean(d_hat * scaled, axis=-1, keepdims=True))
    return inverse * (d_hat - first - scaled * second)

def reference(features, cotangent, dw_kernel, ln_gain, ln_bias, layer_scale, w_up, w_down):
    margin = KW // 2
    flipped = dw_kernel[::-1, ::-1]

    def region_step(totals, inputs):
        region_x, region_cot = inputs
        num_rows, num_cols = (region_x.shape[0], region_x.shape[1])
        xfloat = region_x.astype(jnp.float32)
        padded = jnp.pad(xfloat, ((margin, margin), (margin, margin), (0, 0)))
        conv_out = depthwise(padded, dw_kernel, num_rows, num_cols)
        scaled, inverse, normed = normalize(conv_out, ln_gain, ln_bias)
        tokens = normed.reshape(-1, D)
        scaled_rows = scaled.reshape(-1, D)
        preact = jnp.dot(tokens, w_up, preferred_element_type=jnp.float32)
        activation, slope = gelu_pair(preact)
        hidden_act = activation.astype(jnp.bfloat16)
        mixed = jnp.dot(hidden_act, w_down, preferred_element_type=jnp.float32)
        result = (xfloat.reshape(-1, D) + layer_scale * mixed).astype(jnp.bfloat16)
        cot_rows = region_cot.reshape(-1, D).astype(jnp.float32)
        d_mixed = (layer_scale * cot_rows).astype(jnp.bfloat16)
        d_hidden = jnp.dot(d_mixed, w_down.T, preferred_element_type=jnp.float32)
        d_pre = (d_hidden * slope).astype(jnp.bfloat16)
        d_norm = jnp.dot(d_pre, w_up.T, preferred_element_type=jnp.float32)
        d_conv = norm_back(d_norm, scaled_rows, inverse.reshape(-1, 1), ln_gain).astype(jnp.bfloat16)
        d_conv = lax.optimization_barrier(d_conv)
        d_grid = d_conv.astype(jnp.float32).reshape(num_rows, num_cols, D)
        pad_grad = jnp.pad(d_grid, ((margin, margin), (margin, margin), (0, 0)))
        d_feat = cot_rows.reshape(num_rows, num_cols, D) + depthwise(pad_grad, flipped, num_rows, num_cols)
        grad_up, grad_down, grad_kernel, grad_gain, grad_bias, grad_scale = totals
        totals = (grad_up + jnp.dot(tokens.T, d_pre, preferred_element_type=jnp.float32), grad_down + jnp.dot(hidden_act.T, d_mixed, preferred_element_type=jnp.float32), grad_kernel + kernel_grad(padded, d_grid), grad_gain + lax.optimization_barrier(jnp.sum(d_norm * scaled_rows, axis=0)), grad_bias + lax.optimization_barrier(jnp.sum(d_norm, axis=0)), grad_scale + lax.optimization_barrier(jnp.sum(cot_rows * mixed, axis=0)))
        return (totals, (result.reshape(num_rows, num_cols, D), d_feat))
    zeros = (jnp.zeros((D, FF), jnp.float32), jnp.zeros((FF, D), jnp.float32), jnp.zeros((KW, KW, D), jnp.float32), jnp.zeros((D,), jnp.float32), jnp.zeros((D,), jnp.float32), jnp.zeros((D,), jnp.float32))
    totals, outputs = lax.scan(region_step, zeros, (features, cotangent))
    regions = float(N_DP)
    return (outputs[0], outputs[1], totals[0] / regions, totals[1] / regions, totals[2] / regions, totals[3] / regions, totals[4] / regions, totals[5] / regions)
```

```python
import functools
import math

import jax
import jax.numpy as jnp
from jax import lax
from jax.experimental import pallas as pl
from jax.experimental.pallas import tpu as pltpu
from jax.sharding import PartitionSpec as P

F32, BF16 = jnp.float32, jnp.bfloat16
LANES = 128
EDGE = 8


def gelu_pair(preact):
    cumulative = 0.5 * (1.0 + lax.erf(preact * (1.0 / math.sqrt(2.0))))
    density = jnp.exp(-0.5 * preact * preact) * (1.0 / math.sqrt(2.0 * math.pi))
    return (preact * cumulative, cumulative + preact * density)


def remote(src, dst, send_sem, recv_sem, device):
    return pltpu.make_async_remote_copy(
        src_ref=src,
        dst_ref=dst,
        send_sem=send_sem,
        recv_sem=recv_sem,
        device_id=device,
        device_id_type=pl.DeviceIdType.MESH,
    )


def grid_of(chips):
    across = max(k for k in range(1, chips + 1) if chips % k == 0 and k * k <= chips)
    return chips // across, across


def block_kernel(
    sizes,
    x_hbm, cot_hbm, kern_hbm, gain_hbm, bias_hbm, scale_hbm, wup_hbm, wdown_hbm,
    res_ref, dfeat_ref, gup_ref, gdown_ref, gkern_ref, ggain_ref, gbias_ref, gscale_ref,
    x_ref, cot_ref, kern_ref, gain_ref, bias_ref, scale_ref, wup_ref, wdown_ref,
    xpad, gpad, halo_x, halo_g, conv, scaled_ref, dconv, wout, upg, tok, dmx, hid, dpre,
    part_n, part_m, r1n, r1m, chip_n, chip_m, r2n, r2m, own_n, own_m,
    gpart, gsend, grecv, fsend, frecv, dscale, small, ar1, ar2, ar3,
    in_s, hx_s, hx_r, hg_s, hg_r, w_s, w_r, dm_s, dm_r, tk_s, tk_r,
    an_s, an_r, am_s, am_r, bn_s, bn_r, bm_s, bm_r,
    gz_s, gz_r, fi_s, fi_r, s1_s, s1_r, s2_s, s2_r, s3_s, s3_r,
):
    n_dp, n_sp, rows, cols, width, taps = sizes
    chips, share = n_dp // 2, n_dp // n_sp
    down_n, across_n = grid_of(chips)
    margin = taps // 2
    pixels = rows * cols
    half = pixels // 2
    hidden = wdown_ref.shape[0]
    d, s = lax.axis_index("dp"), lax.axis_index("space")
    chip, core = d // 2, lax.rem(d, 2)
    chip_r, chip_c = chip // across_n, lax.rem(chip, across_n)
    sibling = (chip * 2 + (1 - core), s)
    home = d // share
    place = lax.rem(d, share)
    inside = (home == s).astype(jnp.int32)
    mean_by = 1.0 / n_dp

    pairs = (
        (cot_hbm, cot_ref), (scale_hbm, scale_ref), (x_hbm, x_ref), (wup_hbm, wup_ref),
        (kern_hbm, kern_ref), (gain_hbm, gain_ref), (bias_hbm, bias_ref), (wdown_hbm, wdown_ref),
    )
    loads = [pltpu.make_async_copy(src, dst, in_s.at[i]) for i, (src, dst) in enumerate(pairs)]
    for load in loads:
        load.start()

    def is_self(b):
        return jnp.logical_and(home == s, place == b)

    def dp_peer(off):
        return lax.rem(d + off, n_dp)

    def sp_peer(off):
        return lax.rem(s + off, n_sp)

    barrier = pltpu.get_barrier_semaphore()

    def greet(device):
        pl.semaphore_signal(barrier, inc=1, device_id=device, device_id_type=pl.DeviceIdType.MESH)

    for off in range(1, n_dp):
        greet((dp_peer(off), s))
    for off in range(1, n_sp):
        greet((d, sp_peer(off)))
    for b in range(share):
        @pl.when(jnp.logical_not(is_self(b)))
        def _():
            greet((s * share + b, home))

    for padded in (xpad, gpad):
        padded[...] = jnp.zeros(padded.shape, F32)
    dscale[...] = jnp.zeros(dscale.shape, F32)
    small[...] = jnp.zeros(small.shape, F32)
    loads[0].wait()
    loads[1].wait()
    dmx[0] = (scale_ref[...] * cot_ref[...].astype(F32)).astype(BF16)
    loads[2].wait()
    xpad[margin:margin + rows, EDGE:EDGE + cols] = x_ref[...].astype(F32)
    loads[3].wait()
    for t in range(n_dp):
        wout[t] = wup_ref[:, t * hidden:(t + 1) * hidden]
    upg[d] = wout[d]
    for load in loads[4:]:
        load.wait()
    pl.semaphore_wait(barrier, (n_dp - 1) + (n_sp - 1) + share - inside)

    has_up, has_down = s > 0, s < n_sp - 1

    def halo_copies(source, halo, send, recv):
        down = remote(source.at[pl.ds(rows - margin, margin)], halo.at[0], send.at[0], recv.at[0], (d, jnp.minimum(s + 1, n_sp - 1)))
        up = remote(source.at[pl.ds(0, margin)], halo.at[1], send.at[1], recv.at[1], (d, jnp.maximum(s - 1, 0)))
        return down, up

    def halo_start(copies):
        pl.when(has_down)(copies[0].start)
        pl.when(has_up)(copies[1].start)

    def halo_land(copies, halo, padded):
        @pl.when(has_up)
        def _():
            copies[0].wait_recv()
            padded[0:margin, EDGE:EDGE + cols] = halo[0].astype(F32)

        @pl.when(has_down)
        def _():
            copies[1].wait_recv()
            padded[rows + margin:, EDGE:EDGE + cols] = halo[1].astype(F32)

    def halo_sent(copies):
        pl.when(has_down)(copies[0].wait_send)
        pl.when(has_up)(copies[1].wait_send)

    def chip_at(dr, dc):
        return lax.rem(chip_r + dr, down_n) * across_n + lax.rem(chip_c + dc, across_n)

    def place_of(dr, dc):
        return (dr % down_n) * across_n + dc % across_n

    row_peers = [(0, dc) for dc in range(1, across_n)]
    col_peers = [(dr, 0) for dr in range(1, down_n)]
    diagonals = [(dr, dc) for dr in range(1, down_n) for dc in range(1, across_n)]
    started = []

    class Spread:
        def __init__(self, buf, send, recv):
            self.buf, self.send, self.recv, self.count = buf, send, recv, 0

        def push(self, slot, h, to_slot, device):
            span = pl.ds(h * half, half)
            copy = remote(self.buf.at[slot, span], self.buf.at[to_slot, span], self.send.at[self.count], self.recv.at[2 * to_slot + h], device)
            self.count += 1
            copy.start()
            started.append(copy)

        def own(self, order):
            for dr, dc in row_peers:
                self.push(0, order, 2 * place_of(0, -dc), (chip_at(dr, dc) * 2 + core, s))
            for dr, dc in col_peers:
                self.push(0, 1 - order, 2 * place_of(-dr, 0), (chip_at(dr, dc) * 2 + core, s))

        def own_sibling(self):
            for h in range(2):
                self.push(0, h, 1, sibling)

        def wait(self, slot, h):
            span = pl.ds(h * half, half)
            remote(self.buf.at[slot, span], self.buf.at[slot, span], self.send.at[0], self.recv.at[2 * slot + h], sibling).wait_recv()

        def relay(self, peers, h):
            for dr, dc in peers:
                at = place_of(dr, dc)
                self.wait(2 * at, h)
                if dr == 0 and h == 0:
                    for over, _ in col_peers:
                        self.push(2 * at, h, 2 * place_of(-over, dc), (chip_at(over, 0) * 2 + core, s))
                if dc == 0 and h == 1:
                    for _, over in row_peers:
                        self.push(2 * at, h, 2 * place_of(dr, -over), (chip_at(0, over) * 2 + core, s))
                self.push(2 * at, h, 2 * at + 1, sibling)

        def first(self):
            self.relay(row_peers, 0)
            self.relay(col_peers, 1)

        def second(self):
            self.relay(row_peers, 1)
            self.relay(col_peers, 0)

        def corner(self):
            for h in range(2):
                self.relay(diagonals, h)

        def ready(self, slot):
            for h in range(2):
                self.wait(slot, h)

    hx = halo_copies(x_ref, halo_x, hx_s, hx_r)
    halo_start(hx)
    dm, tk = Spread(dmx, dm_s, dm_r), Spread(tok, tk_s, tk_r)
    w_out = [remote(wout.at[dp_peer(off)], upg.at[d], w_s.at[off], w_r.at[d], (dp_peer(off), s)) for off in range(1, n_dp)]
    w_in = [remote(wout.at[dp_peer(off)], upg.at[dp_peer(off)], w_s.at[off], w_r.at[dp_peer(off)], sibling) for off in range(1, n_dp)]
    dm.own(0)
    for copy in w_out:
        copy.start()
    dm.own_sibling()
    dm.own(1)

    near = [(a, i) for a in range(taps) for i in range(rows) if 0 <= i + a - margin < rows]
    far = [(a, i) for a in range(taps) for i in range(rows) if not 0 <= i + a - margin < rows]

    def convolve(padded, flip, lanes, some, totals):
        totals = dict(totals)
        for b in range(taps):
            first = EDGE - margin + b
            window = {}
            for a, i in some:
                if i + a not in window:
                    window[i + a] = padded[i + a, first:first + cols, lanes]
                at = (taps - 1 - a, taps - 1 - b) if flip else (a, b)
                term = kern_ref[at[0], at[1]:at[1] + 1, lanes] * window[i + a]
                totals[i] = totals[i] + term if i in totals else term
        return totals

    def lanes_of(c):
        return pl.ds(pl.multiple_of(c * LANES, LANES), LANES)

    far_rows = sorted({i for _, i in far})

    @pl.loop(0, width // LANES)
    def _(c):
        lanes = lanes_of(c)
        for i, value in convolve(xpad, False, lanes, near, {}).items():
            conv[i * cols:(i + 1) * cols, lanes] = value

    halo_land(hx, halo_x, xpad)

    @pl.loop(0, width // LANES)
    def _(c):
        lanes = lanes_of(c)
        for i, value in convolve(xpad, False, lanes, far, {i: conv[i * cols:(i + 1) * cols, lanes] for i in far_rows}).items():
            conv[i * cols:(i + 1) * cols, lanes] = value

    center = conv[...]
    center = center - jnp.mean(center, axis=-1, keepdims=True)
    inverse = lax.rsqrt(jnp.mean(center * center, axis=-1, keepdims=True) + 1e-06)
    normal = center * inverse
    scaled_ref[...] = normal
    tok[0] = (normal * gain_ref[...] + bias_ref[...]).astype(BF16)

    tk.own(0)
    tk.own_sibling()
    dm.first()
    tk.own(1)
    for copy in w_in:
        copy.wait_recv()

    def nn(a, b):
        return lax.dot_general(a, b, (((1,), (0,)), ((), ())), preferred_element_type=F32)

    def nt(a, b):
        return lax.dot_general(a, b, (((1,), (1,)), ((), ())), preferred_element_type=F32)

    def tn(a, b):
        return lax.dot_general(a, b, (((0,), (0,)), ((), ())), preferred_element_type=F32)

    def cross(kind, to):
        buf, got, send, recv = kind
        return remote(buf.at[to], got.at[to], send.at[to], recv.at[to], sibling)

    def home_copy(kind, dr, dc):
        buf, got, send, recv = kind
        to, slot = place_of(dr, dc), place_of(-dr, -dc)
        return remote(buf.at[to], got.at[slot], send.at[to], recv.at[slot], (chip_at(dr, dc) * 2 + core, s))

    cross_n, cross_m = (part_n, r1n, an_s, an_r), (part_m, r1m, am_s, am_r)
    home_n, home_m = (chip_n, r2n, bn_s, bn_r), (chip_m, r2m, bm_s, bm_r)

    def products(slot):
        up = upg[...].reshape(width, hidden)
        activation, slope = gelu_pair(nn(tok[slot], up))
        act = activation.astype(BF16)
        grad = (nt(dmx[slot], wdown_ref[...]) * slope).astype(BF16)
        hid[slot] = act
        dpre[slot] = grad
        mixed = nn(act, wdown_ref[...])
        dscale[...] += jnp.sum(dmx[slot].astype(F32) * mixed, axis=0, keepdims=True)
        return nt(grad, up), mixed

    def process(dr, dc):
        at = place_of(dr, dc)
        dm.ready(2 * at + 1)
        tk.ready(2 * at + 1)
        normed, mixed = products(2 * at + 1)
        part_n[at] = normed.astype(BF16)
        cross(cross_n, at).start()
        part_m[at] = mixed.astype(BF16)
        cross(cross_m, at).start()
        normed, mixed = products(2 * at)
        if at:
            cross(cross_n, at).wait_recv()
            chip_n[at] = (normed + r1n[at].astype(F32)).astype(BF16)
            home_copy(home_n, dr, dc).start()
            cross(cross_m, at).wait_recv()
            chip_m[at] = (mixed + r1m[at].astype(F32)).astype(BF16)
        else:
            own_n[...] = normed
            own_m[...] = mixed

    def weight_grads(first, last):
        flat = ((last - first) * pixels,)
        for which, (left, right) in enumerate(((tok, dpre), (dmx, hid))):
            term = tn(left[first:last].reshape(flat + (width,)), right[first:last].reshape(flat + (hidden,)))
            if first:
                gpart[which] += term
            else:
                gpart[which] = term

    process(0, 0)
    tk.first()
    dm.second()
    tk.second()
    for peer in row_peers + col_peers:
        process(*peer)
    dm.corner()
    tk.corner()
    for peer in diagonals:
        process(*peer)
    own_n[...] += r1n_own(cross, cross_n, r1n)
    own_m[...] += r1n_own(cross, cross_m, r1m)
    strip = width // n_sp
    part_rows = strip // share

    def plane_copy(which, off, landing):
        to = sp_peer(off)
        slot = to if landing else s
        return remote(gsend.at[which, to], grecv.at[which, slot], gz_s.at[which, off], gz_r.at[which, slot], (d, to))

    weight_grads(0, n_dp)
    for which in range(2):
        for k in range(n_sp):
            gsend[which, k] = gpart[which, k * strip:(k + 1) * strip].astype(BF16)
        for off in range(1, n_sp):
            plane_copy(which, off, False).start()

    others = row_peers + col_peers + diagonals

    def arrive(got, send, recv, own):
        total = own[...]
        for peer in others:
            at = place_of(*peer)
            remote(got.at[at], got.at[at], send.at[at], recv.at[at], sibling).wait_recv()
            total = total + got[at].astype(F32)
        return total

    d_norm = arrive(r2n, bn_s, bn_r, own_n)
    for peer in others:
        home_copy(home_m, *peer).start()
    normal = scaled_ref[...]
    d_hat = d_norm * gain_ref[...]
    lead = jnp.mean(d_hat, axis=-1, keepdims=True)
    second = jnp.mean(d_hat * normal, axis=-1, keepdims=True)
    dconv[...] = (inverse * (d_hat - lead - normal * second)).astype(BF16).reshape(rows, cols, width)
    hg = halo_copies(dconv, halo_g, hg_s, hg_r)
    halo_start(hg)
    gpad[margin:margin + rows, EDGE:EDGE + cols] = dconv[...].astype(F32)

    per = small.shape[1]
    count = taps * taps

    def put(row, lanes, value):
        small[row // per, row % per:row % per + 1, lanes] = value

    everything = slice(None)
    put(count, everything, jnp.sum(d_norm * normal, axis=0, keepdims=True))
    put(count + 1, everything, jnp.sum(d_norm, axis=0, keepdims=True))
    put(count + 2, everything, dscale[...] / scale_ref[...])

    @pl.loop(0, width // LANES)
    def _(c):
        lanes = lanes_of(c)
        upstream = gpad[margin:margin + rows, EDGE:EDGE + cols, lanes]
        for b in range(taps):
            first = EDGE - margin + b
            window = xpad[:, first:first + cols, lanes]
            for a in range(taps):
                product = jnp.sum(window[a:a + rows] * upstream, axis=0)
                put(a * taps + b, lanes, jnp.sum(product, axis=0, keepdims=True))

    s1_out = [remote(small.at[dp_peer(off)], ar1.at[d], s1_s.at[off], s1_r.at[d], (dp_peer(off), s)) for off in range(1, n_dp)]
    s1_in = [remote(small.at[dp_peer(off)], ar1.at[dp_peer(off)], s1_s.at[off], s1_r.at[dp_peer(off)], sibling) for off in range(1, n_dp)]
    for copy in s1_out:
        copy.start()
    ar1[d] = small[d]

    @pl.loop(0, width // LANES)
    def _(c):
        lanes = lanes_of(c)
        cot = {i: cot_ref[i * cols:(i + 1) * cols, lanes].astype(F32) for i in range(rows)}
        for i, value in convolve(gpad, True, lanes, near, cot).items():
            dfeat_ref[i, :, lanes] = value

    for copy in s1_in:
        copy.wait_recv()
    ar2[s] = jnp.sum(ar1[...], axis=0)
    s2_out = [remote(ar2.at[s], ar2.at[s], s2_s.at[off], s2_r.at[s], (d, sp_peer(off))) for off in range(1, n_sp)]
    s2_in = [remote(ar2.at[s], ar2.at[sp_peer(off)], s2_s.at[off], s2_r.at[sp_peer(off)], (d, sp_peer(off))) for off in range(1, n_sp)]
    for copy in s2_out:
        copy.start()

    halo_land(hg, halo_g, gpad)

    @pl.loop(0, width // LANES)
    def _(c):
        lanes = lanes_of(c)
        for i, value in convolve(gpad, True, lanes, far, {i: dfeat_ref[i, :, lanes] for i in far_rows}).items():
            dfeat_ref[i, :, lanes] = value

    def owner_copy(which, b):
        return remote(fsend.at[which, b], frecv.at[which, place], fi_s.at[which, b], fi_r.at[which, place], (s * share + b, home))

    for which in range(2):
        total = gpart[which, pl.ds(pl.multiple_of(s * strip, strip), strip)]
        for off in range(1, n_sp):
            plane_copy(which, off, True).wait_recv()
            total = total + grecv[which, sp_peer(off)].astype(F32)
        for b in range(share):
            fsend[which, b] = total[b * part_rows:(b + 1) * part_rows].astype(BF16)
            pl.when(jnp.logical_not(is_self(b)))(owner_copy(which, b).start)

            @pl.when(is_self(b))
            def _():
                frecv[which, b] = fsend[which, b]

    for copy in s2_in:
        copy.wait_recv()
    ar3[d] = jnp.sum(ar2[...], axis=0) * mean_by
    s3_out = [remote(ar3.at[d], ar3.at[d], s3_s.at[off], s3_r.at[d], (dp_peer(off), s)) for off in range(1, n_dp)]
    s3_in = [remote(ar3.at[d], ar3.at[dp_peer(off)], s3_s.at[off], s3_r.at[dp_peer(off)], sibling) for off in range(1, n_dp)]
    for copy in s3_out:
        copy.start()

    mixed = arrive(r2m, bm_s, bm_r, own_m)
    res_ref[...] = (x_ref[...].reshape(pixels, width).astype(F32) + scale_ref[...] * mixed).astype(BF16).reshape(rows, cols, width)

    for which, out in enumerate((gup_ref, gdown_ref)):
        for b in range(share):
            landed = remote(fsend.at[which, b], frecv.at[which, b], fi_s.at[which, b], fi_r.at[which, b], sibling)
            pl.when(jnp.logical_not(is_self(b)))(landed.wait_recv)
        for b in range(share):
            out[:, b * hidden:(b + 1) * hidden] = frecv[which, b].astype(F32) * mean_by

    for copy in s3_in:
        copy.wait_recv()

    def take(row):
        return ar3[row // per, row % per:row % per + 1]

    for a in range(taps):
        for b in range(taps):
            gkern_ref[a, b:b + 1] = take(a * taps + b)
    ggain_ref[...] = take(count)
    gbias_ref[...] = take(count + 1)
    gscale_ref[...] = take(count + 2)

    halo_sent(hx)
    halo_sent(hg)
    for group in (started, w_out, s1_out, s2_out, s3_out):
        for copy in group:
            copy.wait_send()
    for which in range(2):
        for off in range(1, n_sp):
            plane_copy(which, off, False).wait_send()
        for b in range(share):
            pl.when(jnp.logical_not(is_self(b)))(owner_copy(which, b).wait_send)

    for at in range(chips):
        cross(cross_n, at).wait_send()
        cross(cross_m, at).wait_send()
    for peer in others:
        home_copy(home_n, *peer).wait_send()
        home_copy(home_m, *peer).wait_send()


def r1n_own(cross, kind, got):
    cross(kind, 0).wait_recv()
    return got[0].astype(F32)


def finish_kernel(*refs):
    n = (len(refs) - 1) // 2
    copies = [pltpu.make_async_copy(refs[i], refs[n + i], refs[-1].at[i]) for i in range(n)]
    for copy in copies:
        copy.start()
    for copy in copies:
        copy.wait()


def finish(arrays):
    return pl.pallas_call(
        finish_kernel,
        out_shape=tuple(jax.ShapeDtypeStruct(a.shape, a.dtype) for a in arrays),
        in_specs=[pl.BlockSpec(memory_space=pltpu.VMEM)] * len(arrays),
        out_specs=(pl.BlockSpec(memory_space=pltpu.HBM),) * len(arrays),
        scratch_shapes=[pltpu.SemaphoreType.DMA((len(arrays),))],
        compiler_params=pltpu.CompilerParams(vmem_limit_bytes=4 << 20),
    )(*arrays)


def local(features, cotangent, dw_kernel, ln_gain, ln_bias, layer_scale, w_up, w_down):
    n_dp, n_sp = lax.axis_size("dp"), lax.axis_size("space")
    _, rows, cols, width = features.shape
    taps = dw_kernel.shape[0]
    margin = taps // 2
    pixels = rows * cols
    hidden = w_down.shape[0]
    chips, share = n_dp // 2, n_dp // n_sp
    strip = width // n_sp
    part_rows = strip // share
    count = taps * taps
    per = -(-(count + 3) // n_dp)
    blocks = (n_dp, w_up.shape[0], hidden)
    padded = (rows + 2 * margin, cols + 2 * EDGE, width)
    dma = lambda k: pltpu.SemaphoreType.DMA((k,))
    vm = pltpu.VMEM
    operands = (
        features[0],
        cotangent[0].reshape(pixels, width),
        dw_kernel,
        ln_gain.reshape(1, width),
        ln_bias.reshape(1, width),
        layer_scale.reshape(1, width),
        w_up,
        w_down,
    )
    operands = tuple(pltpu.with_memory_space_constraint(a, pltpu.HBM) for a in operands)
    scratch = [vm(a.shape, a.dtype) for a in operands]
    scratch += [
        vm(padded, F32), vm(padded, F32),
        vm((2, margin, cols, width), BF16), vm((2, margin, cols, width), BF16),
        vm((pixels, width), F32), vm((pixels, width), F32), vm((rows, cols, width), BF16),
        vm(blocks, BF16), vm(blocks, BF16),
        vm((n_dp, pixels, width), BF16), vm((n_dp, pixels, width), BF16),
        vm((n_dp, pixels, hidden), BF16), vm((n_dp, pixels, hidden), BF16),
    ]
    scratch += [vm((chips, pixels, width), BF16)] * 8
    scratch += [vm((pixels, width), F32)] * 2
    scratch += [
        vm((2, width, hidden), F32),
        vm((2, n_sp, strip, hidden), BF16), vm((2, n_sp, strip, hidden), BF16),
        vm((2, share, part_rows, hidden), BF16), vm((2, share, part_rows, hidden), BF16),
        vm((1, width), F32),
        vm((n_dp, per, width), F32), vm((n_dp, per, width), F32),
        vm((n_sp, per, width), F32), vm((n_dp, per, width), F32),
    ]
    scratch += [dma(len(operands))] + [dma(2)] * 4 + [dma(n_dp)] * 2 + [dma(2 * n_dp)] * 4 + [dma(chips)] * 8
    pair = lambda k: pltpu.SemaphoreType.DMA((2, k))
    scratch += [pair(n_sp)] * 2 + [pair(share)] * 2 + [dma(n_dp)] * 2 + [dma(n_sp)] * 2 + [dma(n_dp)] * 2
    outputs = pl.pallas_call(
        functools.partial(block_kernel, (n_dp, n_sp, rows, cols, width, taps)),
        out_shape=(
            vm((rows, cols, width), BF16),
            vm((rows, cols, width), F32),
            vm((part_rows, share * hidden), F32),
            vm((part_rows, share * hidden), F32),
            vm((taps, taps, width), F32),
        )
        + (vm((1, width), F32),) * 3,
        in_specs=[pl.BlockSpec(memory_space=pltpu.HBM)] * 8,
        out_specs=(pl.BlockSpec(memory_space=pltpu.VMEM),) * 8,
        scratch_shapes=scratch,
        compiler_params=pltpu.CompilerParams(
            collective_id=0, has_side_effects=True, vmem_limit_bytes=40 << 20
        ),
    )(*operands)
    result, d_feat, grad_up, grad_down, kernel_sum, gain_sum, bias_sum, scale_sum = finish(outputs)
    return (
        result[None],
        d_feat[None],
        grad_up,
        grad_down.T,
        kernel_sum,
        gain_sum[0],
        bias_sum[0],
        scale_sum[0],
    )


def solution(mesh):
    in_specs = (
        P("dp", "space", None, None),
        P("dp", "space", None, None),
        P(),
        P(),
        P(),
        P(),
        P("dp", None),
        P("dp", None),
    )
    out_specs = (
        P("dp", "space", None, None),
        P("dp", "space", None, None),
        P("dp", "space"),
        P("space", "dp"),
        P(),
        P(),
        P(),
        P(),
    )
    return jax.shard_map(local, mesh=mesh, in_specs=in_specs, out_specs=out_specs, check_vma=False)
```

```python
import functools
import math

import jax
import jax.numpy as jnp
from jax import lax
from jax.experimental import pallas as pl
from jax.experimental.pallas import tpu as pltpu
from jax.sharding import PartitionSpec as P

F32, BF16 = jnp.float32, jnp.bfloat16
LANES = 128
EDGE = 8


def gelu_pair(preact):
    cumulative = 0.5 * (1.0 + lax.erf(preact * (1.0 / math.sqrt(2.0))))
    density = jnp.exp(-0.5 * preact * preact) * (1.0 / math.sqrt(2.0 * math.pi))
    return (preact * cumulative, cumulative + preact * density)


def remote(src, dst, send_sem, recv_sem, device):
    return pltpu.make_async_remote_copy(
        src_ref=src,
        dst_ref=dst,
        send_sem=send_sem,
        recv_sem=recv_sem,
        device_id=device,
        device_id_type=pl.DeviceIdType.MESH,
    )


def grid_of(chips):
    across = max(k for k in range(1, chips + 1) if chips % k == 0 and k * k <= chips)
    return chips // across, across


def block_kernel(
    sizes,
    x_hbm, cot_hbm, kern_hbm, gain_hbm, bias_hbm, scale_hbm, wup_hbm, wdown_hbm,
    res_ref, dfeat_ref, gup_ref, gdown_ref, gkern_ref, ggain_ref, gbias_ref, gscale_ref,
    x_ref, cot_ref, kern_ref, gain_ref, bias_ref, scale_ref, wup_ref,
    xpad, gpad, halo_x, halo_g, conv, scaled_ref, dconv, wout, upg, wdn, tok, dmx, hid, dpre,
    chip_n, chip_m, r2n, r2m, own_n, own_m,
    gpart, gswap, gback, gsend, grecv, gown, fsend, frecv, dscale, small, ar1, ar2, ar3,
    in_s, hx_s, hx_r, hg_s, hg_r, w_s, w_r, wd_s, wd_r, dm_s, dm_r, tk_s, tk_r,
    bn_s, bn_r, bm_s, bm_r,
    gx_s, gx_r, gz_s, gz_r, fi_s, fi_r, s1_s, s1_r, s2_s, s2_r, s3_s, s3_r,
):
    n_dp, n_sp, rows, cols, width, taps = sizes
    chips, share = n_dp // 2, n_dp // n_sp
    down_n, across_n = grid_of(chips)
    margin = taps // 2
    pixels = rows * cols
    half = pixels // 2
    hidden = wdown_hbm.shape[0]
    d, s = lax.axis_index("dp"), lax.axis_index("space")
    chip, core = d // 2, lax.rem(d, 2)
    chip_r, chip_c = chip // across_n, lax.rem(chip, across_n)
    sibling = (chip * 2 + (1 - core), s)
    home = d // share
    place = lax.rem(d, share)
    inside = (home == s).astype(jnp.int32)
    mean_by = 1.0 / n_dp

    pairs = (
        (cot_hbm, cot_ref), (scale_hbm, scale_ref), (x_hbm, x_ref), (wup_hbm, wup_ref),
        (kern_hbm, kern_ref), (gain_hbm, gain_ref), (bias_hbm, bias_ref), (wdown_hbm, wdn.at[core]),
    )
    loads = [pltpu.make_async_copy(src, dst, in_s.at[i]) for i, (src, dst) in enumerate(pairs)]
    for load in loads:
        load.start()

    def is_self(b):
        return jnp.logical_and(home == s, place == b)

    def dp_peer(off):
        return lax.rem(d + off, n_dp)

    def sp_peer(off):
        return lax.rem(s + off, n_sp)

    barrier = pltpu.get_barrier_semaphore()

    def greet(device):
        pl.semaphore_signal(barrier, inc=1, device_id=device, device_id_type=pl.DeviceIdType.MESH)

    for off in range(1, n_dp):
        greet((dp_peer(off), s))
    for off in range(1, n_sp):
        greet((d, sp_peer(off)))
    for b in range(share):
        @pl.when(jnp.logical_not(is_self(b)))
        def _():
            greet((s * share + b, home))

    for padded in (xpad, gpad):
        padded[...] = jnp.zeros(padded.shape, F32)
    dscale[...] = jnp.zeros(dscale.shape, F32)
    small[...] = jnp.zeros(small.shape, F32)
    loads[0].wait()
    loads[1].wait()
    dmx[0] = (scale_ref[...] * cot_ref[...].astype(F32)).astype(BF16)
    loads[2].wait()
    xpad[margin:margin + rows, EDGE:EDGE + cols] = x_ref[...].astype(F32)
    loads[3].wait()
    for t in range(n_dp):
        wout[t // 2, t % 2] = wup_ref[:, t * hidden:(t + 1) * hidden]
    upg[d] = wout[chip]
    for load in loads[4:]:
        load.wait()
    pl.semaphore_wait(barrier, (n_dp - 1) + (n_sp - 1) + share - inside)

    has_up, has_down = s > 0, s < n_sp - 1

    def halo_copies(source, halo, send, recv):
        down = remote(source.at[pl.ds(rows - margin, margin)], halo.at[0], send.at[0], recv.at[0], (d, jnp.minimum(s + 1, n_sp - 1)))
        up = remote(source.at[pl.ds(0, margin)], halo.at[1], send.at[1], recv.at[1], (d, jnp.maximum(s - 1, 0)))
        return down, up

    def halo_start(copies):
        pl.when(has_down)(copies[0].start)
        pl.when(has_up)(copies[1].start)

    def halo_land(copies, halo, padded):
        @pl.when(has_up)
        def _():
            copies[0].wait_recv()
            padded[0:margin, EDGE:EDGE + cols] = halo[0].astype(F32)

        @pl.when(has_down)
        def _():
            copies[1].wait_recv()
            padded[rows + margin:, EDGE:EDGE + cols] = halo[1].astype(F32)

    def halo_sent(copies):
        pl.when(has_down)(copies[0].wait_send)
        pl.when(has_up)(copies[1].wait_send)

    def chip_at(dr, dc):
        return lax.rem(chip_r + dr, down_n) * across_n + lax.rem(chip_c + dc, across_n)

    def place_of(dr, dc):
        return (dr % down_n) * across_n + dc % across_n

    row_peers = [(0, dc) for dc in range(1, across_n)]
    col_peers = [(dr, 0) for dr in range(1, down_n)]
    diagonals = [(dr, dc) for dr in range(1, down_n) for dc in range(1, across_n)]
    started = []

    class Spread:
        def __init__(self, buf, send, recv):
            self.buf, self.send, self.recv, self.count = buf, send, recv, 0

        def push(self, slot, h, to_slot, dr, dc):
            span = pl.ds(h * half, half)
            copy = remote(self.buf.at[slot, span], self.buf.at[to_slot, span], self.send.at[self.count], self.recv.at[2 * to_slot + h], (chip_at(dr, dc) * 2 + core, s))
            self.count += 1
            copy.start()
            started.append(copy)

        def own(self, order):
            for dr, dc in row_peers:
                self.push(0, order, place_of(0, -dc), dr, dc)
            for dr, dc in col_peers:
                self.push(0, 1 - order, place_of(-dr, 0), dr, dc)

        def wait(self, slot, h):
            span = pl.ds(h * half, half)
            remote(self.buf.at[slot, span], self.buf.at[slot, span], self.send.at[0], self.recv.at[2 * slot + h], sibling).wait_recv()

        def first(self):
            for dr, dc in row_peers:
                self.wait(place_of(dr, dc), 0)
                for over, _ in col_peers:
                    self.push(place_of(dr, dc), 0, place_of(-over, dc), over, 0)
            for dr, dc in col_peers:
                self.wait(place_of(dr, dc), 1)
                for _, over in row_peers:
                    self.push(place_of(dr, dc), 1, place_of(dr, -over), 0, over)

        def second(self, dr, dc):
            self.wait(place_of(dr, dc), 1 if dr == 0 else 0)

        def corner(self, dr, dc):
            for h in range(2):
                self.wait(place_of(dr, dc), h)

    hx = halo_copies(x_ref, halo_x, hx_s, hx_r)
    halo_start(hx)
    dm, tk = Spread(dmx, dm_s, dm_r), Spread(tok, tk_s, tk_r)
    wd_out = remote(wdn.at[core], wdn.at[core], wd_s.at[0], wd_r.at[0], sibling)
    wd_in = remote(wdn.at[1 - core], wdn.at[1 - core], wd_s.at[0], wd_r.at[0], sibling)

    def w_pass(source, index):
        copy = remote(upg.at[source], upg.at[source], w_s.at[index], w_r.at[source], sibling)
        copy.start()
        started.append(copy)

    def w_land(source):
        remote(upg.at[source], upg.at[source], w_s.at[0], w_r.at[source], sibling).wait_recv()

    for i, off in enumerate(range(1, chips)):
        other = lax.rem(chip + off, chips)
        copy = remote(wout.at[other], upg.at[d], w_s.at[i], w_r.at[d], (other * 2 + core, s))
        copy.start()
        started.append(copy)
    wd_out.start()
    w_pass(d, chips - 1)
    dm.own(0)
    dm.own(1)

    near = [(a, i) for a in range(taps) for i in range(rows) if 0 <= i + a - margin < rows]
    far = [(a, i) for a in range(taps) for i in range(rows) if not 0 <= i + a - margin < rows]

    def convolve(padded, flip, lanes, some, totals):
        totals = dict(totals)
        for b in range(taps):
            first = EDGE - margin + b
            window = {}
            for a, i in some:
                if i + a not in window:
                    window[i + a] = padded[i + a, first:first + cols, lanes]
                at = (taps - 1 - a, taps - 1 - b) if flip else (a, b)
                term = kern_ref[at[0], at[1]:at[1] + 1, lanes] * window[i + a]
                totals[i] = totals[i] + term if i in totals else term
        return totals

    def lanes_of(c):
        return pl.ds(pl.multiple_of(c * LANES, LANES), LANES)

    far_rows = sorted({i for _, i in far})

    @pl.loop(0, width // LANES)
    def _(c):
        lanes = lanes_of(c)
        for i, value in convolve(xpad, False, lanes, near, {}).items():
            conv[i * cols:(i + 1) * cols, lanes] = value

    halo_land(hx, halo_x, xpad)

    @pl.loop(0, width // LANES)
    def _(c):
        lanes = lanes_of(c)
        for i, value in convolve(xpad, False, lanes, far, {i: conv[i * cols:(i + 1) * cols, lanes] for i in far_rows}).items():
            conv[i * cols:(i + 1) * cols, lanes] = value

    center = conv[...]
    center = center - jnp.mean(center, axis=-1, keepdims=True)
    inverse = lax.rsqrt(jnp.mean(center * center, axis=-1, keepdims=True) + 1e-06)
    normal = center * inverse
    scaled_ref[...] = normal
    tok[0] = (normal * gain_ref[...] + bias_ref[...]).astype(BF16)

    tk.own(0)
    tk.own(1)
    for off in range(1, chips):
        source = lax.rem(chip + off, chips) * 2 + core
        w_land(source)
        w_pass(source, chips - 1 + off)
    dm.first()
    wd_in.wait_recv()
    for off in range(chips):
        w_land(lax.rem(chip + off, chips) * 2 + 1 - core)

    def nn(a, b):
        return lax.dot_general(a, b, (((1,), (0,)), ((), ())), preferred_element_type=F32)

    def nt(a, b):
        return lax.dot_general(a, b, (((1,), (1,)), ((), ())), preferred_element_type=F32)

    def tn(a, b):
        return lax.dot_general(a, b, (((0,), (0,)), ((), ())), preferred_element_type=F32)

    def home_copy(kind, dr, dc):
        buf, got, send, recv = kind
        to, slot = place_of(dr, dc), place_of(-dr, -dc)
        return remote(buf.at[to], got.at[slot], send.at[to], recv.at[slot], (chip_at(dr, dc) * 2 + core, s))

    home_n, home_m = (chip_n, r2n, bn_s, bn_r), (chip_m, r2m, bm_s, bm_r)

    def process(dr, dc):
        at = place_of(dr, dc)
        mixed, normed = None, None
        for j in range(2):
            up = upg[:, j].reshape(width, hidden)
            activation, slope = gelu_pair(nn(tok[at], up))
            act = activation.astype(BF16)
            grad = (nt(dmx[at], wdn[j]) * slope).astype(BF16)
            hid[j, at] = act
            dpre[j, at] = grad
            normed_j, mixed_j = nt(grad, up), nn(act, wdn[j])
            normed = normed_j if normed is None else normed + normed_j
            mixed = mixed_j if mixed is None else mixed + mixed_j
        if at:
            chip_n[at] = normed.astype(BF16)
            home_copy(home_n, dr, dc).start()
            chip_m[at] = mixed.astype(BF16)
        else:
            own_n[...] = normed
            own_m[...] = mixed
        dscale[...] += jnp.sum(dmx[at].astype(F32) * mixed, axis=0, keepdims=True)

    process(0, 0)
    tk.first()
    for peer in row_peers + col_peers:
        dm.second(*peer)
        tk.second(*peer)
        process(*peer)
    for peer in diagonals:
        dm.corner(*peer)
        tk.corner(*peer)
        process(*peer)
    strip = width // n_sp
    part_rows = strip // share

    def plane_copy(which, off, landing):
        to = sp_peer(off)
        slot = to if landing else s
        return remote(gsend.at[which, to], grecv.at[which, slot], gz_s.at[which, off], gz_r.at[which, slot], (d, to))

    def swap_copy(which, k):
        return remote(gswap.at[which, k], gback.at[which, k], gx_s.at[which, k], gx_r.at[which, k], sibling)

    flat = (chips * pixels,)
    for which, (left, right) in enumerate(((tok, dpre), (dmx, hid))):
        tall = left[...].reshape(flat + (width,))
        for j in range(2):
            gpart[which, j] = tn(tall, right[j].reshape(flat + (hidden,)))
        for off in [*range(1, n_sp), 0]:
            k = sp_peer(off)
            gswap[which, k] = gpart[which, 1 - core, pl.ds(pl.multiple_of(k * strip, strip), strip)].astype(BF16)
            swap_copy(which, k).start()
    for which in range(2):
        for off in [*range(1, n_sp), 0]:
            k = sp_peer(off)
            swap_copy(which, k).wait_recv()
            total = gpart[which, core, pl.ds(pl.multiple_of(k * strip, strip), strip)] + gback[which, k].astype(F32)
            if off:
                gsend[which, k] = total.astype(BF16)
                plane_copy(which, off, False).start()
            else:
                gown[which] = total

    others = row_peers + col_peers + diagonals

    def arrive(got, send, recv, own):
        total = own[...]
        for peer in others:
            at = place_of(*peer)
            remote(got.at[at], got.at[at], send.at[at], recv.at[at], sibling).wait_recv()
            total = total + got[at].astype(F32)
        return total

    d_norm = arrive(r2n, bn_s, bn_r, own_n)
    for peer in row_peers + col_peers:
        home_copy(home_m, *peer).start()
    normal = scaled_ref[...]
    d_hat = d_norm * gain_ref[...]
    lead = jnp.mean(d_hat, axis=-1, keepdims=True)
    second = jnp.mean(d_hat * normal, axis=-1, keepdims=True)
    dconv[...] = (inverse * (d_hat - lead - normal * second)).astype(BF16).reshape(rows, cols, width)
    hg = halo_copies(dconv, halo_g, hg_s, hg_r)
    halo_start(hg)
    gpad[margin:margin + rows, EDGE:EDGE + cols] = dconv[...].astype(F32)

    per = small.shape[1]
    count = taps * taps

    def put(row, lanes, value):
        small[row // per, row % per:row % per + 1, lanes] = value

    everything = slice(None)
    put(count, everything, jnp.sum(d_norm * normal, axis=0, keepdims=True))
    put(count + 1, everything, jnp.sum(d_norm, axis=0, keepdims=True))
    put(count + 2, everything, dscale[...] / scale_ref[...])

    @pl.loop(0, width // LANES)
    def _(c):
        lanes = lanes_of(c)
        upstream = gpad[margin:margin + rows, EDGE:EDGE + cols, lanes]
        for b in range(taps):
            first = EDGE - margin + b
            window = xpad[:, first:first + cols, lanes]
            for a in range(taps):
                product = jnp.sum(window[a:a + rows] * upstream, axis=0)
                put(a * taps + b, lanes, jnp.sum(product, axis=0, keepdims=True))

    s1_out = [remote(small.at[dp_peer(off)], ar1.at[d], s1_s.at[off], s1_r.at[d], (dp_peer(off), s)) for off in range(1, n_dp)]
    s1_in = [remote(small.at[dp_peer(off)], ar1.at[dp_peer(off)], s1_s.at[off], s1_r.at[dp_peer(off)], sibling) for off in range(1, n_dp)]
    for copy in s1_out:
        copy.start()
    for peer in diagonals:
        home_copy(home_m, *peer).start()
    ar1[d] = small[d]

    @pl.loop(0, width // LANES)
    def _(c):
        lanes = lanes_of(c)
        cot = {i: cot_ref[i * cols:(i + 1) * cols, lanes].astype(F32) for i in range(rows)}
        for i, value in convolve(gpad, True, lanes, near, cot).items():
            dfeat_ref[i, :, lanes] = value

    for copy in s1_in:
        copy.wait_recv()
    ar2[s] = jnp.sum(ar1[...], axis=0)
    s2_out = [remote(ar2.at[s], ar2.at[s], s2_s.at[off], s2_r.at[s], (d, sp_peer(off))) for off in range(1, n_sp)]
    s2_in = [remote(ar2.at[s], ar2.at[sp_peer(off)], s2_s.at[off], s2_r.at[sp_peer(off)], (d, sp_peer(off))) for off in range(1, n_sp)]
    for copy in s2_out:
        copy.start()

    halo_land(hg, halo_g, gpad)

    @pl.loop(0, width // LANES)
    def _(c):
        lanes = lanes_of(c)
        for i, value in convolve(gpad, True, lanes, far, {i: dfeat_ref[i, :, lanes] for i in far_rows}).items():
            dfeat_ref[i, :, lanes] = value

    def owner_copy(which, b):
        return remote(fsend.at[which, b], frecv.at[which, place], fi_s.at[which, b], fi_r.at[which, place], (s * share + b, home))

    for which in range(2):
        total = gown[which]
        for off in range(1, n_sp):
            plane_copy(which, off, True).wait_recv()
            total = total + grecv[which, sp_peer(off)].astype(F32)
        for b in range(share):
            fsend[which, b] = total[b * part_rows:(b + 1) * part_rows].astype(BF16)
            pl.when(jnp.logical_not(is_self(b)))(owner_copy(which, b).start)

            @pl.when(is_self(b))
            def _():
                frecv[which, b] = fsend[which, b]

    for copy in s2_in:
        copy.wait_recv()
    ar3[d] = jnp.sum(ar2[...], axis=0) * mean_by
    s3_out = [remote(ar3.at[d], ar3.at[d], s3_s.at[off], s3_r.at[d], (dp_peer(off), s)) for off in range(1, n_dp)]
    s3_in = [remote(ar3.at[d], ar3.at[dp_peer(off)], s3_s.at[off], s3_r.at[dp_peer(off)], sibling) for off in range(1, n_dp)]
    for copy in s3_out:
        copy.start()

    mixed = arrive(r2m, bm_s, bm_r, own_m)
    res_ref[...] = (x_ref[...].reshape(pixels, width).astype(F32) + scale_ref[...] * mixed).astype(BF16).reshape(rows, cols, width)

    for which, out in enumerate((gup_ref, gdown_ref)):
        for b in range(share):
            landed = remote(fsend.at[which, b], frecv.at[which, b], fi_s.at[which, b], fi_r.at[which, b], sibling)
            pl.when(jnp.logical_not(is_self(b)))(landed.wait_recv)
        for b in range(share):
            out[:, b * hidden:(b + 1) * hidden] = frecv[which, b].astype(F32) * mean_by

    for copy in s3_in:
        copy.wait_recv()

    def take(row):
        return ar3[row // per, row % per:row % per + 1]

    for a in range(taps):
        for b in range(taps):
            gkern_ref[a, b:b + 1] = take(a * taps + b)
    ggain_ref[...] = take(count)
    gbias_ref[...] = take(count + 1)
    gscale_ref[...] = take(count + 2)

    halo_sent(hx)
    halo_sent(hg)
    wd_out.wait_send()
    for group in (started, s1_out, s2_out, s3_out):
        for copy in group:
            copy.wait_send()
    for which in range(2):
        for off in range(1, n_sp):
            plane_copy(which, off, False).wait_send()
        for b in range(share):
            pl.when(jnp.logical_not(is_self(b)))(owner_copy(which, b).wait_send)

    for which in range(2):
        for k in range(n_sp):
            swap_copy(which, k).wait_send()
    for peer in others:
        home_copy(home_n, *peer).wait_send()
        home_copy(home_m, *peer).wait_send()


def finish_kernel(*refs):
    n = (len(refs) - 1) // 2
    copies = [pltpu.make_async_copy(refs[i], refs[n + i], refs[-1].at[i]) for i in range(n)]
    for copy in copies:
        copy.start()
    for copy in copies:
        copy.wait()


def finish(arrays):
    return pl.pallas_call(
        finish_kernel,
        out_shape=tuple(jax.ShapeDtypeStruct(a.shape, a.dtype) for a in arrays),
        in_specs=[pl.BlockSpec(memory_space=pltpu.VMEM)] * len(arrays),
        out_specs=(pl.BlockSpec(memory_space=pltpu.HBM),) * len(arrays),
        scratch_shapes=[pltpu.SemaphoreType.DMA((len(arrays),))],
        compiler_params=pltpu.CompilerParams(vmem_limit_bytes=4 << 20),
    )(*arrays)


def local(features, cotangent, dw_kernel, ln_gain, ln_bias, layer_scale, w_up, w_down):
    n_dp, n_sp = lax.axis_size("dp"), lax.axis_size("space")
    _, rows, cols, width = features.shape
    taps = dw_kernel.shape[0]
    margin = taps // 2
    pixels = rows * cols
    hidden = w_down.shape[0]
    chips, share = n_dp // 2, n_dp // n_sp
    strip = width // n_sp
    part_rows = strip // share
    count = taps * taps
    per = -(-(count + 3) // n_dp)
    block = (2, w_up.shape[0], hidden)
    padded = (rows + 2 * margin, cols + 2 * EDGE, width)
    dma = lambda k: pltpu.SemaphoreType.DMA((k,))
    vm = pltpu.VMEM
    operands = (
        features[0],
        cotangent[0].reshape(pixels, width),
        dw_kernel,
        ln_gain.reshape(1, width),
        ln_bias.reshape(1, width),
        layer_scale.reshape(1, width),
        w_up,
        w_down,
    )
    operands = tuple(pltpu.with_memory_space_constraint(a, pltpu.HBM) for a in operands)
    scratch = [vm(a.shape, a.dtype) for a in operands[:-1]]
    scratch += [
        vm(padded, F32), vm(padded, F32),
        vm((2, margin, cols, width), BF16), vm((2, margin, cols, width), BF16),
        vm((pixels, width), F32), vm((pixels, width), F32), vm((rows, cols, width), BF16),
        vm((chips,) + block, BF16), vm((n_dp,) + block, BF16), vm((2, hidden, width), BF16),
        vm((chips, pixels, width), BF16), vm((chips, pixels, width), BF16),
        vm((2, chips, pixels, hidden), BF16), vm((2, chips, pixels, hidden), BF16),
    ]
    scratch += [vm((chips, pixels, width), BF16)] * 4
    scratch += [vm((pixels, width), F32)] * 2
    scratch += [
        vm((2, 2, width, hidden), F32),
    ]
    scratch += [vm((2, n_sp, strip, hidden), BF16)] * 4
    scratch += [
        vm((2, strip, hidden), F32),
        vm((2, share, part_rows, hidden), BF16), vm((2, share, part_rows, hidden), BF16),
        vm((1, width), F32),
        vm((n_dp, per, width), F32), vm((n_dp, per, width), F32),
        vm((n_sp, per, width), F32), vm((n_dp, per, width), F32),
    ]
    scratch += [dma(len(operands))] + [dma(2)] * 4 + [dma(n_dp)] * 2 + [dma(1)] * 2 + [dma(n_dp)] * 4 + [dma(chips)] * 4
    pair = lambda k: pltpu.SemaphoreType.DMA((2, k))
    scratch += [pair(n_sp)] * 4 + [pair(share)] * 2 + [dma(n_dp)] * 2 + [dma(n_sp)] * 2 + [dma(n_dp)] * 2
    outputs = pl.pallas_call(
        functools.partial(block_kernel, (n_dp, n_sp, rows, cols, width, taps)),
        out_shape=(
            vm((rows, cols, width), BF16),
            vm((rows, cols, width), F32),
            vm((part_rows, share * hidden), F32),
            vm((part_rows, share * hidden), F32),
            vm((taps, taps, width), F32),
        )
        + (vm((1, width), F32),) * 3,
        in_specs=[pl.BlockSpec(memory_space=pltpu.HBM)] * 8,
        out_specs=(pl.BlockSpec(memory_space=pltpu.VMEM),) * 8,
        scratch_shapes=scratch,
        compiler_params=pltpu.CompilerParams(
            collective_id=0, has_side_effects=True, vmem_limit_bytes=40 << 20
        ),
    )(*operands)
    result, d_feat, grad_up, grad_down, kernel_sum, gain_sum, bias_sum, scale_sum = finish(outputs)
    return (
        result[None],
        d_feat[None],
        grad_up,
        grad_down.T,
        kernel_sum,
        gain_sum[0],
        bias_sum[0],
        scale_sum[0],
    )


def solution(mesh):
    in_specs = (
        P("dp", "space", None, None),
        P("dp", "space", None, None),
        P(),
        P(),
        P(),
        P(),
        P("dp", None),
        P("dp", None),
    )
    out_specs = (
        P("dp", "space", None, None),
        P("dp", "space", None, None),
        P("dp", "space"),
        P("space", "dp"),
        P(),
        P(),
        P(),
        P(),
    )
    return jax.shard_map(local, mesh=mesh, in_specs=in_specs, out_specs=out_specs, check_vma=False)
```

```python
import functools
import math

import jax
import jax.numpy as jnp
from jax import lax
from jax.experimental import pallas as pl
from jax.experimental.pallas import tpu as pltpu
from jax.sharding import PartitionSpec as P

F32, BF16 = jnp.float32, jnp.bfloat16
LANES = 128
EDGE = 8


def gelu_pair(preact):
    cumulative = 0.5 * (1.0 + lax.erf(preact * (1.0 / math.sqrt(2.0))))
    density = jnp.exp(-0.5 * preact * preact) * (1.0 / math.sqrt(2.0 * math.pi))
    return (preact * cumulative, cumulative + preact * density)


def remote(src, dst, send_sem, recv_sem, device):
    return pltpu.make_async_remote_copy(
        src_ref=src,
        dst_ref=dst,
        send_sem=send_sem,
        recv_sem=recv_sem,
        device_id=device,
        device_id_type=pl.DeviceIdType.MESH,
    )


def grid_of(chips):
    across = max(k for k in range(1, chips + 1) if chips % k == 0 and k * k <= chips)
    return chips // across, across


def block_kernel(
    sizes,
    x_hbm, cot_hbm, kern_hbm, gain_hbm, bias_hbm, scale_hbm, wup_hbm, wdown_hbm,
    res_ref, dfeat_ref, gup_ref, gdown_ref, gkern_ref, ggain_ref, gbias_ref, gscale_ref,
    x_ref, cot_ref, kern_ref, gain_ref, bias_ref, scale_ref, wup_ref,
    xpad, gpad, halo_x, halo_g, conv, scaled_ref, dconv, wout, upg, wdn, tok, dmx, hid, dpre,
    chip_n, chip_m, r2n, r2m, own_n, own_m,
    gpart, gswap, gback, gsend, grecv, gown, ghold, gpass, fsend, frecv, dscale, small, ar1, ar2, ar3,
    in_s, hx_s, hx_r, hg_s, hg_r, w_s, w_r, wd_s, wd_r, dm_s, dm_r, tk_s, tk_r,
    bn_s, bn_r, bm_s, bm_r,
    gx_s, gx_r, gz_s, gz_r, gp_r, fi_s, fi_r, s1_s, s1_r, s2_s, s2_r, s3_s, s3_r,
):
    n_dp, n_sp, rows, cols, width, taps = sizes
    chips, share = n_dp // 2, n_dp // n_sp
    down_n, across_n = grid_of(chips)
    margin = taps // 2
    pixels = rows * cols
    half = pixels // 2
    hidden = wdown_hbm.shape[0]
    d, s = lax.axis_index("dp"), lax.axis_index("space")
    chip, core = d // 2, lax.rem(d, 2)
    chip_r, chip_c = chip // across_n, lax.rem(chip, across_n)
    sibling = (chip * 2 + (1 - core), s)
    home = d // share
    place = lax.rem(d, share)
    inside = (home == s).astype(jnp.int32)
    mean_by = 1.0 / n_dp

    pairs = (
        (cot_hbm, cot_ref), (scale_hbm, scale_ref), (x_hbm, x_ref), (wup_hbm, wup_ref),
        (kern_hbm, kern_ref), (gain_hbm, gain_ref), (bias_hbm, bias_ref), (wdown_hbm, wdn.at[core]),
    )
    loads = [pltpu.make_async_copy(src, dst, in_s.at[i]) for i, (src, dst) in enumerate(pairs)]
    for load in loads:
        load.start()

    def is_self(b):
        return jnp.logical_and(home == s, place == b)

    def dp_peer(off):
        return lax.rem(d + off, n_dp)

    def sp_peer(off):
        return lax.rem(s + off, n_sp)

    barrier = pltpu.get_barrier_semaphore()

    def greet(device):
        pl.semaphore_signal(barrier, inc=1, device_id=device, device_id_type=pl.DeviceIdType.MESH)

    for off in range(1, n_dp):
        greet((dp_peer(off), s))
    for off in range(1, n_sp):
        greet((d, sp_peer(off)))
    for b in range(share):
        @pl.when(jnp.logical_not(is_self(b)))
        def _():
            greet((s * share + b, home))

    for padded in (xpad, gpad):
        padded[...] = jnp.zeros(padded.shape, F32)
    dscale[...] = jnp.zeros(dscale.shape, F32)
    small[...] = jnp.zeros(small.shape, F32)
    for edge, unused in ((0, n_sp - 1), (n_sp - 1, 0)):
        @pl.when(s == edge)
        def _():
            grecv[:, unused] = jnp.zeros((2,) + grecv.shape[2:], BF16)
    loads[0].wait()
    loads[1].wait()
    dmx[0] = (scale_ref[...] * cot_ref[...].astype(F32)).astype(BF16)
    loads[2].wait()
    xpad[margin:margin + rows, EDGE:EDGE + cols] = x_ref[...].astype(F32)
    loads[3].wait()
    for t in range(n_dp):
        wout[t // 2, t % 2] = wup_ref[:, t * hidden:(t + 1) * hidden]
    upg[d] = wout[chip]
    for load in loads[4:]:
        load.wait()
    pl.semaphore_wait(barrier, (n_dp - 1) + (n_sp - 1) + share - inside)

    has_up, has_down = s > 0, s < n_sp - 1

    def halo_copies(source, halo, send, recv):
        down = remote(source.at[pl.ds(rows - margin, margin)], halo.at[0], send.at[0], recv.at[0], (d, jnp.minimum(s + 1, n_sp - 1)))
        up = remote(source.at[pl.ds(0, margin)], halo.at[1], send.at[1], recv.at[1], (d, jnp.maximum(s - 1, 0)))
        return down, up

    def halo_start(copies):
        pl.when(has_down)(copies[0].start)
        pl.when(has_up)(copies[1].start)

    def halo_land(copies, halo, padded):
        @pl.when(has_up)
        def _():
            copies[0].wait_recv()
            padded[0:margin, EDGE:EDGE + cols] = halo[0].astype(F32)

        @pl.when(has_down)
        def _():
            copies[1].wait_recv()
            padded[rows + margin:, EDGE:EDGE + cols] = halo[1].astype(F32)

    def halo_sent(copies):
        pl.when(has_down)(copies[0].wait_send)
        pl.when(has_up)(copies[1].wait_send)

    def chip_at(dr, dc):
        return lax.rem(chip_r + dr, down_n) * across_n + lax.rem(chip_c + dc, across_n)

    def place_of(dr, dc):
        return (dr % down_n) * across_n + dc % across_n

    row_peers = [(0, dc) for dc in range(1, across_n)]
    col_peers = [(dr, 0) for dr in range(1, down_n)]
    diagonals = [(dr, dc) for dr in range(1, down_n) for dc in range(1, across_n)]
    started = []

    class Spread:
        def __init__(self, buf, send, recv):
            self.buf, self.send, self.recv, self.count = buf, send, recv, 0

        def push(self, slot, h, to_slot, dr, dc):
            span = pl.ds(h * half, half)
            copy = remote(self.buf.at[slot, span], self.buf.at[to_slot, span], self.send.at[self.count], self.recv.at[2 * to_slot + h], (chip_at(dr, dc) * 2 + core, s))
            self.count += 1
            copy.start()
            started.append(copy)

        def own(self, order):
            for dr, dc in row_peers:
                self.push(0, order, place_of(0, -dc), dr, dc)
            for dr, dc in col_peers:
                self.push(0, 1 - order, place_of(-dr, 0), dr, dc)

        def wait(self, slot, h):
            span = pl.ds(h * half, half)
            remote(self.buf.at[slot, span], self.buf.at[slot, span], self.send.at[0], self.recv.at[2 * slot + h], sibling).wait_recv()

        def first(self):
            for dr, dc in row_peers:
                self.wait(place_of(dr, dc), 0)
                for over, _ in col_peers:
                    self.push(place_of(dr, dc), 0, place_of(-over, dc), over, 0)
            for dr, dc in col_peers:
                self.wait(place_of(dr, dc), 1)
                for _, over in row_peers:
                    self.push(place_of(dr, dc), 1, place_of(dr, -over), 0, over)

        def second(self, dr, dc):
            self.wait(place_of(dr, dc), 1 if dr == 0 else 0)

        def corner(self, dr, dc):
            for h in range(2):
                self.wait(place_of(dr, dc), h)

    hx = halo_copies(x_ref, halo_x, hx_s, hx_r)
    halo_start(hx)
    dm, tk = Spread(dmx, dm_s, dm_r), Spread(tok, tk_s, tk_r)
    wd_out = remote(wdn.at[core], wdn.at[core], wd_s.at[0], wd_r.at[0], sibling)
    wd_in = remote(wdn.at[1 - core], wdn.at[1 - core], wd_s.at[0], wd_r.at[0], sibling)

    def w_pass(source, index):
        copy = remote(upg.at[source], upg.at[source], w_s.at[index], w_r.at[source], sibling)
        copy.start()
        started.append(copy)

    def w_land(source):
        remote(upg.at[source], upg.at[source], w_s.at[0], w_r.at[source], sibling).wait_recv()

    for i, off in enumerate(range(1, chips)):
        other = lax.rem(chip + off, chips)
        copy = remote(wout.at[other], upg.at[d], w_s.at[i], w_r.at[d], (other * 2 + core, s))
        copy.start()
        started.append(copy)
    wd_out.start()
    w_pass(d, chips - 1)
    dm.own(0)
    dm.own(1)

    near = [(a, i) for a in range(taps) for i in range(rows) if 0 <= i + a - margin < rows]
    far = [(a, i) for a in range(taps) for i in range(rows) if not 0 <= i + a - margin < rows]

    def convolve(padded, flip, lanes, some, totals):
        totals = dict(totals)
        for b in range(taps):
            first = EDGE - margin + b
            window = {}
            for a, i in some:
                if i + a not in window:
                    window[i + a] = padded[i + a, first:first + cols, lanes]
                at = (taps - 1 - a, taps - 1 - b) if flip else (a, b)
                term = kern_ref[at[0], at[1]:at[1] + 1, lanes] * window[i + a]
                totals[i] = totals[i] + term if i in totals else term
        return totals

    def lanes_of(c):
        return pl.ds(pl.multiple_of(c * LANES, LANES), LANES)

    far_rows = sorted({i for _, i in far})

    @pl.loop(0, width // LANES)
    def _(c):
        lanes = lanes_of(c)
        for i, value in convolve(xpad, False, lanes, near, {}).items():
            conv[i * cols:(i + 1) * cols, lanes] = value

    halo_land(hx, halo_x, xpad)

    @pl.loop(0, width // LANES)
    def _(c):
        lanes = lanes_of(c)
        for i, value in convolve(xpad, False, lanes, far, {i: conv[i * cols:(i + 1) * cols, lanes] for i in far_rows}).items():
            conv[i * cols:(i + 1) * cols, lanes] = value

    center = conv[...]
    center = center - jnp.mean(center, axis=-1, keepdims=True)
    inverse = lax.rsqrt(jnp.mean(center * center, axis=-1, keepdims=True) + 1e-06)
    normal = center * inverse
    scaled_ref[...] = normal
    tok[0] = (normal * gain_ref[...] + bias_ref[...]).astype(BF16)

    tk.own(0)
    tk.own(1)
    for off in range(1, chips):
        source = lax.rem(chip + off, chips) * 2 + core
        w_land(source)
        w_pass(source, chips - 1 + off)
    dm.first()
    wd_in.wait_recv()
    for off in range(chips):
        w_land(lax.rem(chip + off, chips) * 2 + 1 - core)

    def nn(a, b):
        return lax.dot_general(a, b, (((1,), (0,)), ((), ())), preferred_element_type=F32)

    def nt(a, b):
        return lax.dot_general(a, b, (((1,), (1,)), ((), ())), preferred_element_type=F32)

    def tn(a, b):
        return lax.dot_general(a, b, (((0,), (0,)), ((), ())), preferred_element_type=F32)

    def home_copy(kind, dr, dc):
        buf, got, send, recv = kind
        to, slot = place_of(dr, dc), place_of(-dr, -dc)
        return remote(buf.at[to], got.at[slot], send.at[to], recv.at[slot], (chip_at(dr, dc) * 2 + core, s))

    home_n = (chip_n, r2n, bn_s, bn_r)

    def home_half(dr, dc, h):
        to, slot, span = place_of(dr, dc), place_of(-dr, -dc), pl.ds(h * half, half)
        return remote(chip_m.at[to, span], r2m.at[slot, span], bm_s.at[2 * to + h], bm_r.at[2 * slot + h], (chip_at(dr, dc) * 2 + core, s))

    def weight_grads(which, first, last):
        left, right = ((tok, dpre), (dmx, hid))[which]
        flat = ((last - first) * pixels,)
        tall = left[first:last].reshape(flat + (width,))
        for j in range(2):
            term = tn(tall, right[j, first:last].reshape(flat + (hidden,)))
            gpart[which, j] = gpart[which, j] + term if first else term

    def process(dr, dc):
        at = place_of(dr, dc)
        mixed, normed = None, None
        for j in range(2):
            up = upg[:, j].reshape(width, hidden)
            activation, slope = gelu_pair(nn(tok[at], up))
            act = activation.astype(BF16)
            grad = (nt(dmx[at], wdn[j]) * slope).astype(BF16)
            hid[j, at] = act
            dpre[j, at] = grad
            normed_j, mixed_j = nt(grad, up), nn(act, wdn[j])
            normed = normed_j if normed is None else normed + normed_j
            mixed = mixed_j if mixed is None else mixed + mixed_j
        if at:
            chip_n[at] = normed.astype(BF16)
            home_copy(home_n, dr, dc).start()
            chip_m[at] = mixed.astype(BF16)
        else:
            own_n[...] = normed
            own_m[...] = mixed
        dscale[...] += jnp.sum(dmx[at].astype(F32) * mixed, axis=0, keepdims=True)

    process(0, 0)
    tk.first()
    for peer in row_peers + col_peers:
        dm.second(*peer)
        tk.second(*peer)
        process(*peer)
    done = {0} | {place_of(*peer) for peer in row_peers + col_peers}
    lead = next(at for at in range(chips + 1) if at not in done)
    for which in range(2):
        weight_grads(which, 0, lead)
    for peer in diagonals:
        dm.corner(*peer)
        tk.corner(*peer)
        process(*peer)
    strip = width // n_sp
    part_rows = strip // share

    bend = n_sp >= 4
    relay_dev = jnp.logical_or(s == 1, s == n_sp - 2)
    far_of_relay = jnp.where(s == 1, n_sp - 1, 0)
    near_edge = jnp.where(s == 0, 1, n_sp - 2)

    def far_pair(k):
        return jnp.logical_and(bend, abs(s - k) == n_sp - 1)

    def relays(k):
        return jnp.logical_and(jnp.logical_and(bend, relay_dev), k == far_of_relay)

    def plane_copy(which, k):
        return remote(gsend.at[which, k], grecv.at[which, s], gz_s.at[which, k], gz_r.at[which, s], (d, k))

    def bent_copy(which, k):
        return remote(gsend.at[which, k], gpass.at[which], gz_s.at[which, k], gp_r.at[which], (d, near_edge))

    def plane_land(which, k):
        remote(gsend.at[which, k], grecv.at[which, k], gz_s.at[which, k], gz_r.at[which, k], (d, k)).wait_recv()

    def toward(i):
        return lax.rem(s + jnp.where(2 * s < n_sp, n_sp - i, i), n_sp)

    def swap_copy(which, k):
        return remote(gswap.at[which, k], gback.at[which, k], gx_s.at[which, k], gx_r.at[which, k], sibling)

    for which in range(2):
        if lead < chips:
            weight_grads(which, lead, chips)
        for i in [*range(1, n_sp), 0]:
            k = toward(i)
            gswap[which, k] = gpart[which, 1 - core, pl.ds(pl.multiple_of(k * strip, strip), strip)].astype(BF16)
            swap_copy(which, k).start()
    for which in range(2):
        for i in [*range(1, n_sp), 0]:
            k = toward(i)
            swap_copy(which, k).wait_recv()
            total = gpart[which, core, pl.ds(pl.multiple_of(k * strip, strip), strip)] + gback[which, k].astype(F32)
            if not i:
                gown[which] = total
                continue
            gsend[which, k] = total.astype(BF16)

            @pl.when(relays(k))
            def _():
                ghold[which] = total

            @pl.when(far_pair(k))
            def _():
                bent_copy(which, k).start()

            @pl.when(jnp.logical_not(jnp.logical_or(far_pair(k), relays(k))))
            def _():
                plane_copy(which, k).start()
    def relay(which):
        if bend:
            @pl.when(relay_dev)
            def _():
                remote(gsend.at[which, s], gpass.at[which], gz_s.at[which, s], gp_r.at[which], sibling).wait_recv()
                gsend[which, far_of_relay] = (ghold[which] + gpass[which].astype(F32)).astype(BF16)
                plane_copy(which, far_of_relay).start()

    others = row_peers + col_peers + diagonals

    d_norm = own_n[...]
    for peer in others:
        at = place_of(*peer)
        remote(r2n.at[at], r2n.at[at], bn_s.at[at], bn_r.at[at], sibling).wait_recv()
        d_norm = d_norm + r2n[at].astype(F32)
    for peer in row_peers + col_peers:
        home_half(*peer, 0).start()
    normal = scaled_ref[...]
    d_hat = d_norm * gain_ref[...]
    lead = jnp.mean(d_hat, axis=-1, keepdims=True)
    second = jnp.mean(d_hat * normal, axis=-1, keepdims=True)
    dconv[...] = (inverse * (d_hat - lead - normal * second)).astype(BF16).reshape(rows, cols, width)
    hg = halo_copies(dconv, halo_g, hg_s, hg_r)
    halo_start(hg)
    gpad[margin:margin + rows, EDGE:EDGE + cols] = dconv[...].astype(F32)

    per = small.shape[1]
    count = taps * taps

    def put(row, lanes, value):
        small[row // per, row % per:row % per + 1, lanes] = value

    everything = slice(None)
    put(count, everything, jnp.sum(d_norm * normal, axis=0, keepdims=True))
    put(count + 1, everything, jnp.sum(d_norm, axis=0, keepdims=True))
    put(count + 2, everything, dscale[...] / scale_ref[...])

    relay(0)
    @pl.loop(0, width // LANES)
    def _(c):
        lanes = lanes_of(c)
        upstream = gpad[margin:margin + rows, EDGE:EDGE + cols, lanes]
        for b in range(taps):
            first = EDGE - margin + b
            window = xpad[:, first:first + cols, lanes]
            for a in range(taps):
                product = jnp.sum(window[a:a + rows] * upstream, axis=0)
                put(a * taps + b, lanes, jnp.sum(product, axis=0, keepdims=True))

    s1_out = [remote(small.at[dp_peer(off)], ar1.at[d], s1_s.at[off], s1_r.at[d], (dp_peer(off), s)) for off in range(1, n_dp)]
    s1_in = [remote(small.at[dp_peer(off)], ar1.at[dp_peer(off)], s1_s.at[off], s1_r.at[dp_peer(off)], sibling) for off in range(1, n_dp)]
    for copy in s1_out:
        copy.start()
    for peer in row_peers + col_peers:
        home_half(*peer, 1).start()
    for peer in diagonals:
        for h in range(2):
            home_half(*peer, h).start()
    ar1[d] = small[d]

    relay(1)
    @pl.loop(0, width // LANES)
    def _(c):
        lanes = lanes_of(c)
        cot = {i: cot_ref[i * cols:(i + 1) * cols, lanes].astype(F32) for i in range(rows)}
        for i, value in convolve(gpad, True, lanes, near, cot).items():
            dfeat_ref[i, :, lanes] = value

    for copy in s1_in:
        copy.wait_recv()
    ar2[s] = jnp.sum(ar1[...], axis=0)
    s2_out = [remote(ar2.at[s], ar2.at[s], s2_s.at[off], s2_r.at[s], (d, sp_peer(off))) for off in range(1, n_sp)]
    s2_in = [remote(ar2.at[s], ar2.at[sp_peer(off)], s2_s.at[off], s2_r.at[sp_peer(off)], (d, sp_peer(off))) for off in range(1, n_sp)]
    for copy in s2_out:
        copy.start()

    def owner_copy(which, b):
        return remote(fsend.at[which, b], frecv.at[which, place], fi_s.at[which, b], fi_r.at[which, place], (s * share + b, home))

    def owner_send(which):
        total = gown[which]
        for off in range(1, n_sp):
            k = sp_peer(off)

            @pl.when(jnp.logical_not(far_pair(k)))
            def _():
                plane_land(which, k)

            total = total + grecv[which, k].astype(F32)
        for b in range(share):
            fsend[which, b] = total[b * part_rows:(b + 1) * part_rows].astype(BF16)
            pl.when(jnp.logical_not(is_self(b)))(owner_copy(which, b).start)

            @pl.when(is_self(b))
            def _():
                frecv[which, b] = fsend[which, b]

    owner_send(0)
    owner_send(1)

    for copy in s2_in:
        copy.wait_recv()
    ar3[d] = jnp.sum(ar2[...], axis=0) * mean_by
    s3_out = [remote(ar3.at[d], ar3.at[d], s3_s.at[off], s3_r.at[d], (dp_peer(off), s)) for off in range(1, n_dp)]
    s3_in = [remote(ar3.at[d], ar3.at[dp_peer(off)], s3_s.at[off], s3_r.at[dp_peer(off)], sibling) for off in range(1, n_dp)]
    for copy in s3_out:
        copy.start()

    halo_land(hg, halo_g, gpad)

    @pl.loop(0, width // LANES)
    def _(c):
        lanes = lanes_of(c)
        for i, value in convolve(gpad, True, lanes, far, {i: dfeat_ref[i, :, lanes] for i in far_rows}).items():
            dfeat_ref[i, :, lanes] = value

    mixed = own_m[...]
    for peer in others:
        at = place_of(*peer)
        for h in range(2):
            span = pl.ds(h * half, half)
            remote(r2m.at[at, span], r2m.at[at, span], bm_s.at[2 * at + h], bm_r.at[2 * at + h], sibling).wait_recv()
        mixed = mixed + r2m[at].astype(F32)
    res_ref[...] = (x_ref[...].reshape(pixels, width).astype(F32) + scale_ref[...] * mixed).astype(BF16).reshape(rows, cols, width)

    for which, out in enumerate((gup_ref, gdown_ref)):
        for b in range(share):
            landed = remote(fsend.at[which, b], frecv.at[which, b], fi_s.at[which, b], fi_r.at[which, b], sibling)
            pl.when(jnp.logical_not(is_self(b)))(landed.wait_recv)
        for b in range(share):
            out[:, b * hidden:(b + 1) * hidden] = frecv[which, b].astype(F32) * mean_by

    for copy in s3_in:
        copy.wait_recv()

    def take(row):
        return ar3[row // per, row % per:row % per + 1]

    for a in range(taps):
        for b in range(taps):
            gkern_ref[a, b:b + 1] = take(a * taps + b)
    ggain_ref[...] = take(count)
    gbias_ref[...] = take(count + 1)
    gscale_ref[...] = take(count + 2)

    halo_sent(hx)
    halo_sent(hg)
    wd_out.wait_send()
    for group in (started, s1_out, s2_out, s3_out):
        for copy in group:
            copy.wait_send()
    for which in range(2):
        for off in range(1, n_sp):
            plane_copy(which, sp_peer(off)).wait_send()
        for b in range(share):
            pl.when(jnp.logical_not(is_self(b)))(owner_copy(which, b).wait_send)

    for which in range(2):
        for k in range(n_sp):
            swap_copy(which, k).wait_send()
    for peer in others:
        home_copy(home_n, *peer).wait_send()
        for h in range(2):
            home_half(*peer, h).wait_send()


def finish_kernel(*refs):
    n = (len(refs) - 1) // 2
    copies = [pltpu.make_async_copy(refs[i], refs[n + i], refs[-1].at[i]) for i in range(n)]
    for copy in copies:
        copy.start()
    for copy in copies:
        copy.wait()


def finish(arrays):
    return pl.pallas_call(
        finish_kernel,
        out_shape=tuple(jax.ShapeDtypeStruct(a.shape, a.dtype) for a in arrays),
        in_specs=[pl.BlockSpec(memory_space=pltpu.VMEM)] * len(arrays),
        out_specs=(pl.BlockSpec(memory_space=pltpu.HBM),) * len(arrays),
        scratch_shapes=[pltpu.SemaphoreType.DMA((len(arrays),))],
        compiler_params=pltpu.CompilerParams(vmem_limit_bytes=4 << 20),
    )(*arrays)


def local(features, cotangent, dw_kernel, ln_gain, ln_bias, layer_scale, w_up, w_down):
    n_dp, n_sp = lax.axis_size("dp"), lax.axis_size("space")
    _, rows, cols, width = features.shape
    taps = dw_kernel.shape[0]
    margin = taps // 2
    pixels = rows * cols
    hidden = w_down.shape[0]
    chips, share = n_dp // 2, n_dp // n_sp
    strip = width // n_sp
    part_rows = strip // share
    count = taps * taps
    per = -(-(count + 3) // n_dp)
    block = (2, w_up.shape[0], hidden)
    padded = (rows + 2 * margin, cols + 2 * EDGE, width)
    dma = lambda k: pltpu.SemaphoreType.DMA((k,))
    vm = pltpu.VMEM
    operands = (
        features[0],
        cotangent[0].reshape(pixels, width),
        dw_kernel,
        ln_gain.reshape(1, width),
        ln_bias.reshape(1, width),
        layer_scale.reshape(1, width),
        w_up,
        w_down,
    )
    operands = tuple(pltpu.with_memory_space_constraint(a, pltpu.HBM) for a in operands)
    scratch = [vm(a.shape, a.dtype) for a in operands[:-1]]
    scratch += [
        vm(padded, F32), vm(padded, F32),
        vm((2, margin, cols, width), BF16), vm((2, margin, cols, width), BF16),
        vm((pixels, width), F32), vm((pixels, width), F32), vm((rows, cols, width), BF16),
        vm((chips,) + block, BF16), vm((n_dp,) + block, BF16), vm((2, hidden, width), BF16),
        vm((chips, pixels, width), BF16), vm((chips, pixels, width), BF16),
        vm((2, chips, pixels, hidden), BF16), vm((2, chips, pixels, hidden), BF16),
    ]
    scratch += [vm((chips, pixels, width), BF16)] * 4
    scratch += [vm((pixels, width), F32)] * 2
    scratch += [
        vm((2, 2, width, hidden), F32),
    ]
    scratch += [vm((2, n_sp, strip, hidden), BF16)] * 4
    scratch += [
        vm((2, strip, hidden), F32), vm((2, strip, hidden), F32), vm((2, strip, hidden), BF16),
        vm((2, share, part_rows, hidden), BF16), vm((2, share, part_rows, hidden), BF16),
        vm((1, width), F32),
        vm((n_dp, per, width), F32), vm((n_dp, per, width), F32),
        vm((n_sp, per, width), F32), vm((n_dp, per, width), F32),
    ]
    scratch += [dma(len(operands))] + [dma(2)] * 4 + [dma(n_dp)] * 2 + [dma(1)] * 2 + [dma(n_dp)] * 4 + [dma(chips)] * 2 + [dma(n_dp)] * 2
    pair = lambda k: pltpu.SemaphoreType.DMA((2, k))
    scratch += [pair(n_sp)] * 4 + [dma(2)] + [pair(share)] * 2 + [dma(n_dp)] * 2 + [dma(n_sp)] * 2 + [dma(n_dp)] * 2
    outputs = pl.pallas_call(
        functools.partial(block_kernel, (n_dp, n_sp, rows, cols, width, taps)),
        out_shape=(
            vm((rows, cols, width), BF16),
            vm((rows, cols, width), F32),
            vm((part_rows, share * hidden), F32),
            vm((part_rows, share * hidden), F32),
            vm((taps, taps, width), F32),
        )
        + (vm((1, width), F32),) * 3,
        in_specs=[pl.BlockSpec(memory_space=pltpu.HBM)] * 8,
        out_specs=(pl.BlockSpec(memory_space=pltpu.VMEM),) * 8,
        scratch_shapes=scratch,
        compiler_params=pltpu.CompilerParams(
            collective_id=0, has_side_effects=True, vmem_limit_bytes=40 << 20
        ),
    )(*operands)
    result, d_feat, grad_up, grad_down, kernel_sum, gain_sum, bias_sum, scale_sum = finish(outputs)
    return (
        result[None],
        d_feat[None],
        grad_up,
        grad_down.T,
        kernel_sum,
        gain_sum[0],
        bias_sum[0],
        scale_sum[0],
    )


def solution(mesh):
    in_specs = (
        P("dp", "space", None, None),
        P("dp", "space", None, None),
        P(),
        P(),
        P(),
        P(),
        P("dp", None),
        P("dp", None),
    )
    out_specs = (
        P("dp", "space", None, None),
        P("dp", "space", None, None),
        P("dp", "space"),
        P("space", "dp"),
        P(),
        P(),
        P(),
        P(),
    )
    return jax.shard_map(local, mesh=mesh, in_specs=in_specs, out_specs=out_specs, check_vma=False)
```
